512 devices in a mesh: req: 64 (over z_lo, x, core), tp: 8 (over y, z_hi).
Axes of the slice: x: 4, y: 4, z: 16 (z_hi: 2, z_lo: 8; z = z_hi * 8 + z_lo), core: 2. Of those that a mesh axis runs over, the one named last changes fastest.
Arguments:
- block_x: bfloat16 [24576, 4096], P('req', 'tp'), may hold values from -400 to 400
- decode_x: bfloat16 [2048, 4096], P('req', 'tp'), may hold values from -400 to 400
- gain: bfloat16 [4096], replicated, may hold values from 0.099609375 to 1.8984375
- w_qkv: bfloat16 [4096, 6144], P(None, 'tp'), may hold values from -0.09375 to 0.09375
- ctx_cache: bfloat16 [65536, 2048], P('req', 'tp'), may hold values from -500 to 500
- prompt_cache: bfloat16 [32768, 2048], P('req', 'tp'), may hold values from -500 to 500
- tail_pool: bfloat16 [131072, 2048], P('req', 'tp'), may hold values from -500 to 500
- page_table: int32 [64, 128], P('req'), may hold values from 0 to 127, each once within a row
- tail_len: int32 [64, 32], P('req'), may hold values from 1 to 64, 1280 in all within a row
- block_offset: int32 [64], P('req'), may hold values from 256 to 1024, as said below
- move_mask: int32 [1], replicated, may hold values from 1 to 63
Outputs:
- block_out: bfloat16 [24576, 4096], P('req', 'tp')
- decode_out: bfloat16 [2048, 4096], P('req', 'tp')
The draws below stay inside these ranges and needn't reach their ends.
Inputs may be any that keep to these rules, and one draw needn't show every extreme that they name: `page_table`: each row is a permutation of 0 to 127. `tail_len`: each row sums to 1280 and holds 64 at least once. `block_offset`: some request has exactly 1024 in every draw.
All inputs are finite; a program needn't handle non-finite values.
Results may differ from the reference program's by a relative error of at most 0.0065.
The reference program's roundings to bfloat16 on the way (of `scaled` and `weights`) count: a program that leaves them out, or rounds other values in their place, can miss the bound.
Values may be sent and summed in bfloat16 or wider, within the bound.
A program may use at most 64 MiB of HBM per device.

```python
import math
import jax
import jax.numpy as jnp
import numpy as np
from jax import lax

D = 4096
HEADS = 32
KV_HEADS = 8
HEAD = 128
BLOCK = 384
CTXT = 1024
G = 32
PROMPT = 512
TAIL = 64
PAGE = 16
QPG = 4
POOL = 128
BLOCK_ROWS = 24576
DECODE_ROWS = 2048
CTX_ROWS = 65536
PROMPT_ROWS = 32768
POOL_ROWS = 131072
N_REQ = 64


def activation_draw(key, row_count):
    base = jax.random.normal(jax.random.fold_in(key, 13), (row_count, D), jnp.float32)
    column_scale = jnp.exp(jax.random.uniform(jax.random.fold_in(key, 14), (1, D), jnp.float32, 0.0, math.log(10.0)))
    row_scale = jnp.exp(jax.random.uniform(jax.random.fold_in(key, 15), (row_count, 1), jnp.float32, math.log(0.3), math.log(3.0)))
    return jnp.clip(base * column_scale * row_scale, -400.0, 400.0)


def cache_draw(key, row_count):
    width = KV_HEADS * 2 * HEAD
    base = jax.random.normal(jax.random.fold_in(key, 25), (row_count, width), jnp.float32)
    return jnp.clip(base, -500.0, 500.0)


def draw_block_x(key, part):
    return activation_draw(jax.random.fold_in(key, 101), BLOCK_ROWS).astype(jnp.bfloat16)


def draw_decode_x(key, part):
    return activation_draw(jax.random.fold_in(key, 102), DECODE_ROWS).astype(jnp.bfloat16)


def draw_ctx_cache(key, part):
    return cache_draw(jax.random.fold_in(key, 201), CTX_ROWS).astype(jnp.bfloat16)


def draw_prompt_cache(key, part):
    return cache_draw(jax.random.fold_in(key, 202), PROMPT_ROWS).astype(jnp.bfloat16)


def draw_tail_pool(key, part):
    return cache_draw(jax.random.fold_in(key, 203), POOL_ROWS).astype(jnp.bfloat16)


def draw_block_offset(key, part):
    values = jax.random.randint(jax.random.fold_in(key, 31), (N_REQ,), CTXT // 4, CTXT + 1)
    place = jax.random.randint(jax.random.fold_in(key, 32), (), 0, N_REQ)
    return jnp.where(jnp.arange(N_REQ) == place, CTXT, values).astype(jnp.int32)


def block_levels(rng, extent, cuts, low, high):
    level = 1.0
    for dim, shards_of in cuts:
        steps = jax.random.uniform(jax.random.fold_in(jax.random.fold_in(rng, 6), dim), (shards_of,), jnp.float32, low / len(cuts), high / len(cuts))
        level = level * jnp.repeat(jnp.exp(steps), extent[dim] // shards_of).reshape((-1,) + (1,) * (len(extent) - 1 - dim))
    return level


def profile(count, total, limit, slope):
    portions = [(1 << 20) // math.isqrt(grade ** slope) + 1 for grade in range(2, count + 1)]
    rest, given = total - limit - (count - 1), [1] * (count - 1)
    while rest > 0:
        free = [i for i in range(count - 1) if given[i] < limit]
        pool, budget = sum([portions[i] for i in free]), rest
        for i in free:
            addition = min(limit - given[i], max(1, budget * portions[i] // pool), rest)
            given[i] = given[i] + addition
            rest = rest - addition
    return np.array([limit] + given)


def ragged_sizes(rng, count, total, most, lean):
    if count == 2:
        one = jax.random.randint(rng, (), max(1, total - most), min(most, total - 1) + 1)
        return jnp.stack([one, total - one])
    lengths = jnp.asarray(profile(count, total, most, lean), jnp.int32)
    pairs = (count - 1) // 2
    giver, sink = lengths[1:1 + 2 * pairs:2], lengths[2:2 + 2 * pairs:2]
    room = jnp.minimum(giver - 1, most - sink)
    passed = jax.random.randint(jax.random.fold_in(rng, 1), (pairs,), 0, 1 << 20) % (room + 1)
    lengths = lengths.at[1:1 + 2 * pairs:2].set(giver - passed).at[2:2 + 2 * pairs:2].set(sink + passed)
    return lengths[jax.random.permutation(jax.random.fold_in(rng, 2), count)]


def normal_values(own_key, dims, scale, most, split=(), kind=jnp.bfloat16):
    factor_of = block_levels(own_key, dims, split, -0.22, 0.18) if split else 1.0
    entries = jax.random.normal(own_key, dims, jnp.float32) * scale * factor_of
    return jnp.minimum(jnp.maximum(entries, -most), most).astype(kind)


def setup_inputs(seed: int = 0) -> dict:
    arg_keys = jax.random.split(jax.random.key(seed), 12)
    return {
        "block_x": draw_block_x(jax.random.fold_in(arg_keys[11], 71), 0),
        "decode_x": draw_decode_x(jax.random.fold_in(arg_keys[11], 71), 0),
        "gain": jnp.clip(1.0 + 0.18 * jax.random.normal(arg_keys[2], (D,), jnp.float32), 0.099609375, 1.8984375).astype(jnp.bfloat16),
        "w_qkv": normal_values(arg_keys[3], (D, (HEADS + 2 * KV_HEADS) * HEAD), D ** -0.5, 0.09375, ((1, 8),)),
        "ctx_cache": draw_ctx_cache(jax.random.fold_in(arg_keys[11], 71), 0),
        "prompt_cache": draw_prompt_cache(jax.random.fold_in(arg_keys[11], 71), 0),
        "tail_pool": draw_tail_pool(jax.random.fold_in(arg_keys[11], 71), 0),
        "page_table": jax.vmap(lambda own: jax.random.permutation(own, POOL))(jax.random.split(arg_keys[7], N_REQ)).reshape((N_REQ, POOL)).astype(jnp.int32),
        "tail_len": jax.vmap(lambda own: ragged_sizes(own, G, G * TAIL * 5 // 8, TAIL, 1))(jax.random.split(arg_keys[8], N_REQ)).reshape((N_REQ, G)).astype(jnp.int32),
        "block_offset": draw_block_offset(jax.random.fold_in(arg_keys[11], 71), 0),
        "move_mask": jax.random.randint(arg_keys[10], (1,), 1, N_REQ).astype(jnp.int32),
    }


EPS = 1e-05
THETA = 1000000.0

def rotate(tensor, position):
    middle = tensor.shape[-1] // 2
    column = jnp.arange(middle, dtype=jnp.float32)
    frequency = jnp.power(THETA, -2.0 * column / tensor.shape[-1])
    angle = position * frequency
    cosine = jnp.cos(angle)
    sine = jnp.sin(angle)
    first = tensor[..., :middle]
    second = tensor[..., middle:]
    return jnp.concatenate([first * cosine - second * sine, second * cosine + first * sine], axis=-1)

def project(rows, gain, w_qkv):
    exact = rows.astype(jnp.float32)
    scaled = (exact * gain.astype(jnp.float32)).astype(jnp.bfloat16)
    totals = jnp.dot(scaled, w_qkv, preferred_element_type=jnp.float32)
    squares = lax.optimization_barrier(jnp.sum(exact * exact, axis=1))
    return totals * lax.rsqrt(squares / w_qkv.shape[0] + EPS)[:, None]

def split_heads(projected, position):
    groups = projected.shape[1] // ((QPG + 2) * HEAD)
    shaped = projected.reshape(projected.shape[0], groups, QPG + 2, HEAD)
    rotated = rotate(shaped, position[:, None, None, None])
    queries = rotated[:, :, :QPG].astype(jnp.bfloat16)
    keys_new = rotated[:, :, QPG].astype(jnp.bfloat16)
    values_new = shaped[:, :, QPG + 1].astype(jnp.bfloat16)
    return (queries, keys_new, values_new)

def normalize(scores):
    highest = lax.optimization_barrier(jnp.max(scores, axis=-1, keepdims=True))
    expo = jnp.exp(scores - highest)
    return (expo / lax.optimization_barrier(jnp.sum(expo, axis=-1, keepdims=True))).astype(jnp.bfloat16)

def block_attend(queries, keys_new, values_new, cache, offset):
    rows_count = queries.shape[0]
    groups = queries.shape[1]
    cached = cache.shape[0]
    shaped = cache.reshape(cached, groups, 2, HEAD)
    keys_all = jnp.concatenate([shaped[:, :, 0], keys_new], axis=0).astype(jnp.float32)
    values_all = jnp.concatenate([shaped[:, :, 1], values_new], axis=0).astype(jnp.float32)
    scores = jnp.einsum('ckqd,jkd->kqcj', queries.astype(jnp.float32), keys_all) * HEAD ** (-0.5)
    columns = jnp.arange(cached + rows_count)[None, :]
    row_index = jnp.arange(rows_count)[:, None]
    valid = jnp.where(columns < cached, columns < offset, columns - cached <= row_index)
    scores = jnp.where(valid, scores, -jnp.inf)
    weights = normalize(scores)
    output = jnp.einsum('kqcj,jkd->ckqd', weights.astype(jnp.float32), values_all)
    return output.reshape(rows_count, -1).astype(jnp.bfloat16)

def decode_attend(queries, keys_new, values_new, prompt, tail_cache, tail_counts):
    group_rows = queries.shape[0]
    groups = queries.shape[1]
    prompt_len = prompt.shape[0]
    tail_slots = tail_cache.shape[1]
    prompt_kv = prompt.reshape(prompt_len, groups, 2, HEAD).astype(jnp.float32)
    tail_kv = tail_cache.reshape(group_rows, tail_slots, groups, 2, HEAD).astype(jnp.float32)
    query_f = queries.astype(jnp.float32)
    score_prompt = jnp.einsum('gkqd,jkd->gkqj', query_f, prompt_kv[:, :, 0])
    score_tail = jnp.einsum('gkqd,gtkd->gkqt', query_f, tail_kv[:, :, :, 0])
    live = jnp.arange(tail_slots)[None, None, None, :] < tail_counts[:, None, None, None]
    score_tail = jnp.where(live, score_tail, -jnp.inf)
    score_own = jnp.einsum('gkqd,gkd->gkq', query_f, keys_new.astype(jnp.float32))[..., None]
    scores = jnp.concatenate([score_prompt, score_tail, score_own], axis=-1) * HEAD ** (-0.5)
    weights = normalize(scores).astype(jnp.float32)
    output = jnp.einsum('gkqj,jkd->gkqd', weights[..., :prompt_len], prompt_kv[:, :, 1])
    output = output + jnp.einsum('gkqt,gtkd->gkqd', weights[..., prompt_len:prompt_len + tail_slots], tail_kv[:, :, :, 1])
    output = output + weights[..., -1:] * values_new.astype(jnp.float32)[:, :, None, :]
    return output.reshape(group_rows, -1).astype(jnp.bfloat16)

def reference(block_x, decode_x, gain, w_qkv, ctx_cache, prompt_cache, tail_pool, page_table, tail_len, block_offset, move_mask):
    block_pos = (block_offset[:, None] + jnp.arange(BLOCK, dtype=jnp.int32)[None, :]).reshape(-1).astype(jnp.float32)
    block_q, block_k, block_v = split_heads(project(block_x, gain, w_qkv), block_pos)
    block_q = block_q.reshape(N_REQ, BLOCK, KV_HEADS, QPG, HEAD)
    block_k = block_k.reshape(N_REQ, BLOCK, KV_HEADS, HEAD)
    block_v = block_v.reshape(N_REQ, BLOCK, KV_HEADS, HEAD)
    contexts = ctx_cache.reshape(N_REQ, CTXT, -1)

    def one_block(items):
        return block_attend(items[0], items[1], items[2], items[3], items[4])
    block_out = lax.map(one_block, (block_q, block_k, block_v, contexts, block_offset))
    decode_pos = (PROMPT + tail_len).reshape(-1).astype(jnp.float32)
    dec_q, dec_k, dec_v = split_heads(project(decode_x, gain, w_qkv), decode_pos)
    dec_q = dec_q.reshape(N_REQ, G, KV_HEADS, QPG, HEAD)
    dec_k = dec_k.reshape(N_REQ, G, KV_HEADS, HEAD)
    dec_v = dec_v.reshape(N_REQ, G, KV_HEADS, HEAD)
    pools = tail_pool.reshape(N_REQ, POOL, PAGE, -1)
    tails = jax.vmap(lambda pool_pages, table: jnp.take(pool_pages, table, axis=0))(pools, page_table)
    tails = tails.reshape(N_REQ, G, TAIL, -1)
    prompts = prompt_cache.reshape(N_REQ, PROMPT, -1)

    def one_group(items):
        return decode_attend(items[0], items[1], items[2], items[3], items[4], items[5])
    home_out = lax.map(one_group, (dec_q, dec_k, dec_v, prompts, tails, tail_len))
    source = jnp.bitwise_xor(jnp.arange(N_REQ, dtype=jnp.int32), move_mask[0])
    decode_out = jnp.take(home_out, source, axis=0)
    return (block_out.reshape(N_REQ * BLOCK, -1), decode_out.reshape(N_REQ * G, -1))
```

```python
import jax
import jax.numpy as jnp
from jax import lax
from jax.sharding import PartitionSpec as P

HEAD = 128
QPG = 4


EPS = 1e-05
THETA = 1000000.0


def as_sent(shard):

    def short(part):
        return part.astype(jnp.bfloat16) if part.dtype == jnp.float32 else part

    return jax.tree.map(short, shard)


def from_partner(shard, axis, apart):
    return lax.ppermute(shard, axis, [(i, i ^ 1 << apart) for i in range(lax.axis_size(axis))])


def rotate(tensor, position):
    middle = tensor.shape[-1] // 2
    column = jnp.arange(middle, dtype=jnp.float32)
    frequency = jnp.power(THETA, -2.0 * column / tensor.shape[-1])
    angle = position * frequency
    cosine = jnp.cos(angle)
    sine = jnp.sin(angle)
    first = tensor[..., :middle]
    second = tensor[..., middle:]
    return jnp.concatenate(
        [first * cosine - second * sine, second * cosine + first * sine], axis=-1
    )


def project_rows(rows, gain, w_qkv):
    exact = lax.all_gather(rows, "tp", axis=1, tiled=True).astype(jnp.float32)
    gain_part = gain.astype(jnp.float32)
    scaled = (exact * gain_part).astype(jnp.bfloat16)
    totals = jnp.dot(scaled, w_qkv, preferred_element_type=jnp.float32)
    squares = jnp.sum(exact * exact, axis=1)
    totals, squares = (totals, squares)
    return totals * lax.rsqrt(squares / w_qkv.shape[0] + EPS)[:, None]


def split_heads(projected, position):
    groups = projected.shape[1] // ((QPG + 2) * HEAD)
    shaped = projected.reshape(projected.shape[0], groups, QPG + 2, HEAD)
    rotated = rotate(shaped, position[:, None, None, None])
    queries = rotated[:, :, :QPG].astype(jnp.bfloat16)
    keys_new = rotated[:, :, QPG].astype(jnp.bfloat16)
    values_new = shaped[:, :, QPG + 1].astype(jnp.bfloat16)
    return (queries, keys_new, values_new)


def normalize(scores):
    highest = jnp.max(scores, axis=-1, keepdims=True)
    expo = jnp.exp(scores - highest)
    return (expo / jnp.sum(expo, axis=-1, keepdims=True)).astype(jnp.bfloat16)


def block_attend(queries, keys_new, values_new, cache, offset):
    rows_count = queries.shape[0]
    groups = queries.shape[1]
    cached = cache.shape[0]
    shaped = cache.reshape(cached, groups, 2, HEAD)
    keys_all = jnp.concatenate([shaped[:, :, 0], keys_new], axis=0)
    values_all = jnp.concatenate([shaped[:, :, 1], values_new], axis=0)
    scores = jnp.einsum(
        "ckqd,jkd->kqcj", queries, keys_all, preferred_element_type=jnp.float32
    ) * HEAD ** (-0.5)
    columns = jnp.arange(cached + rows_count)[None, :]
    row_index = jnp.arange(rows_count)[:, None]
    valid = jnp.where(columns < cached, columns < offset, columns - cached <= row_index)
    scores = jnp.where(valid, scores, -jnp.inf)
    weights = normalize(scores)
    output = jnp.einsum("kqcj,jkd->ckqd", weights, values_all, preferred_element_type=jnp.float32)
    return output.reshape(rows_count, -1).astype(jnp.bfloat16)


def decode_attend(queries, keys_new, values_new, prompt, tail_cache, tail_counts):
    group_rows = queries.shape[0]
    groups = queries.shape[1]
    prompt_len = prompt.shape[0]
    tail_slots = tail_cache.shape[1]
    prompt_kv = prompt.reshape(prompt_len, groups, 2, HEAD)
    tail_kv = tail_cache.reshape(group_rows, tail_slots, groups, 2, HEAD)
    score_prompt = jnp.einsum(
        "gkqd,jkd->gkqj", queries, prompt_kv[:, :, 0], preferred_element_type=jnp.float32
    )
    score_tail = jnp.einsum(
        "gkqd,gtkd->gkqt", queries, tail_kv[:, :, :, 0], preferred_element_type=jnp.float32
    )
    live = jnp.arange(tail_slots)[None, None, None, :] < tail_counts[:, None, None, None]
    score_tail = jnp.where(live, score_tail, -jnp.inf)
    score_own = jnp.einsum("gkqd,gkd->gkq", queries, keys_new, preferred_element_type=jnp.float32)[
        ..., None
    ]
    scores = jnp.concatenate([score_prompt, score_tail, score_own], axis=-1) * HEAD ** (-0.5)
    weights = normalize(scores)
    output = jnp.einsum(
        "gkqj,jkd->gkqd",
        weights[..., :prompt_len],
        prompt_kv[:, :, 1],
        preferred_element_type=jnp.float32,
    )
    output = output + jnp.einsum(
        "gkqt,gtkd->gkqd",
        weights[..., prompt_len : prompt_len + tail_slots],
        tail_kv[:, :, :, 1],
        preferred_element_type=jnp.float32,
    )
    output = (
        output
        + weights[..., -1:].astype(jnp.float32) * values_new.astype(jnp.float32)[:, :, None, :]
    )
    return output.reshape(group_rows, -1).astype(jnp.bfloat16)


def attend_all(
    projected, block_pos, tail_counts, block_rows, ctx_cache, offset, prompt, tail_cache
):
    decode_pos = (prompt.shape[0] + tail_counts).astype(jnp.float32)
    positions = jnp.concatenate([block_pos, decode_pos], axis=0)
    queries, keys_new, values_new = split_heads(projected, positions)
    block_out = block_attend(
        queries[:block_rows], keys_new[:block_rows], values_new[:block_rows], ctx_cache, offset
    )
    decode_out = decode_attend(
        queries[block_rows:],
        keys_new[block_rows:],
        values_new[block_rows:],
        prompt,
        tail_cache,
        tail_counts,
    )
    return (block_out, decode_out)


def hop_migrate(payload, bit_index):
    return jax.tree.map(
        lambda part, own: part.astype(own.dtype),
        from_partner(as_sent(payload), "req", bit_index),
        payload,
    )


def relocate(payload, xor_mask, hop_count, mover):
    for bit_index in range(hop_count):
        take_new = jnp.bitwise_and(jnp.right_shift(xor_mask, bit_index), 1) == 1
        swapped = mover(payload, bit_index)
        payload = jax.tree.map(
            lambda stayed, arrived: jnp.where(take_new, arrived, stayed), payload, swapped
        )
    return payload


def per_device(
    block_x,
    decode_x,
    gain,
    w_qkv,
    ctx_cache,
    prompt_cache,
    tail_pool,
    page_table,
    tail_len,
    block_offset,
    move_mask,
):
    block_rows = block_x.shape[0]
    group_rows = decode_x.shape[0]
    cache_width = ctx_cache.shape[1]
    pool_pages = page_table.shape[1]
    tail_cache = jnp.take(tail_pool.reshape(pool_pages, -1, cache_width), page_table[0], axis=0)
    tail_cache = tail_cache.reshape(group_rows, -1, cache_width)
    tail_counts = tail_len[0]
    offset = block_offset[0]
    block_pos = (offset + jnp.arange(block_rows, dtype=jnp.int32)).astype(jnp.float32)
    xor_mask = move_mask[0]
    hop_count = lax.axis_size("req").bit_length() - 1
    projected = project_rows(jnp.concatenate([block_x, decode_x], axis=0), gain, w_qkv)
    block_out, decode_out = attend_all(
        projected,
        block_pos,
        tail_counts,
        block_rows,
        ctx_cache,
        offset,
        prompt_cache,
        tail_cache,
    )
    decode_out = relocate(decode_out, xor_mask, hop_count, hop_migrate)
    return (block_out, decode_out)


def solution(mesh):
    in_specs = (
        P("req", "tp"),
        P("req", "tp"),
        P(),
        P(None, "tp"),
        P("req", "tp"),
        P("req", "tp"),
        P("req", "tp"),
        P("req", None),
        P("req", None),
        P("req"),
        P(),
    )
    out_specs = (P("req", "tp"), P("req", "tp"))
    return jax.shard_map(
        per_device, mesh=mesh, in_specs=in_specs, out_specs=out_specs, check_vma=False
    )
```

```python
import functools
import math

import jax
import jax.numpy as jnp
import numpy as np
from jax import lax
from jax.experimental import pallas as pl
from jax.experimental.pallas import tpu as pltpu
from jax.sharding import PartitionSpec as P

HEAD = 128
QPG = 4
EPS = 1e-05
THETA = 1000000.0
PAGE = 16
MESH = pl.DeviceIdType.MESH
CHUNKS = ((0, 32), (32, 96), (128, 96), (224, 96), (320, 64), (384, 32))
OWN = ((0, 32), (32, 192), (224, 192))
HOPS = 6
MASKED = -1e30
FACTOR = HEAD ** -0.5 * math.log2(math.e)


def where_am_i():
    req = lax.axis_index("req")
    tp = lax.axis_index("tp")
    return req, tp, tp // 2, tp % 2


def layer_kernel(
    block_x, decode_x, gain, w_hbm, ctx_hbm, prompt_hbm, pool_hbm, table, tail_len, offset, mask, freq,
    block_out, decode_out,
    gathered, w, ctx, prompt, pool, place_of, acc, squares, cosines, sines, keys_new, values_new,
    out_rows, moved, landed, local_sem, send_sem, recv_sem,
):
    req, tp, y, zh = where_am_i()
    group_rows = decode_x.shape[0]
    block_rows = block_x.shape[0]
    depth = decode_x.shape[1]
    opposite = (req, tp + 1 - 2 * zh)

    def along_y(step):
        return (req, ((y + step + 4) % 4) * 2 + zh)

    def partner(bit):
        here = (req // (1 << bit)) % 2
        return (req + (1 - 2 * here) * (1 << bit), tp)

    peers = [opposite, along_y(1), along_y(-1)] + [partner(bit) for bit in range(HOPS)]
    barrier = pltpu.get_barrier_semaphore()
    for peer in peers:
        pl.semaphore_signal(barrier, inc=1, device_id=peer, device_id_type=MESH)

    locals_ = [
        pltpu.make_async_copy(decode_x, gathered.at[tp, pl.ds(0, group_rows)], local_sem.at[0]),
        pltpu.make_async_copy(block_x, gathered.at[tp, pl.ds(group_rows, block_rows)], local_sem.at[1]),
        pltpu.make_async_copy(w_hbm, w, local_sem.at[2]),
        pltpu.make_async_copy(pool_hbm, pool, local_sem.at[3]),
        pltpu.make_async_copy(prompt_hbm, prompt, local_sem.at[4]),
        pltpu.make_async_copy(ctx_hbm, ctx, local_sem.at[5]),
    ]
    for copy in locals_:
        copy.start()
    pl.semaphore_wait(barrier, len(peers))

    sent = []

    def send(source, target, device):
        index = len(sent)
        copy = pltpu.make_async_remote_copy(
            src_ref=source, dst_ref=target, send_sem=send_sem.at[index], recv_sem=recv_sem.at[index],
            device_id=device, device_id_type=MESH,
        )
        copy.start()
        sent.append(copy)
        return copy

    def own_rows(start, rows):
        if start < group_rows:
            return decode_x.at[pl.ds(start, rows)]
        return block_x.at[pl.ds(start - group_rows, rows)]

    directions = (1, -1)
    across = [send(own_rows(s, n), gathered.at[tp, pl.ds(s, n)], opposite) for s, n in CHUNKS]
    beside = [
        [send(own_rows(s, n), gathered.at[tp, pl.ds(s, n)], along_y(d)) for d in directions] for s, n in OWN
    ]

    def forward(arrived, start, rows, half):
        copies = []
        for which, d in enumerate(directions):
            arrived[which].wait_recv()
            slot = ((y - d + 4) % 4) * 2 + half
            view = gathered.at[slot, pl.ds(start + which * (rows // 2), rows // 2)]
            copies.append(send(view, view, along_y(d)))
        return copies

    def forward_own(index):
        return forward(beside[index], OWN[index][0], OWN[index][1], zh)

    def spread(index):
        start, rows = CHUNKS[index]
        across[index].wait_recv()
        view = gathered.at[tp + 1 - 2 * zh, pl.ds(start, rows)]
        return [send(view, view, along_y(d)) for d in directions]

    def forward_far(index, arrived):
        return forward(arrived, CHUNKS[index][0], CHUNKS[index][1], 1 - zh)

    def half_product(start, rows, half):
        total = None
        square = None
        for j in range(4):
            slot = 2 * j + half
            exact = gathered[slot, pl.ds(start, rows), :].astype(jnp.float32)
            base = pl.multiple_of(slot * depth, depth)
            scaled = (exact * gain[:, pl.ds(base, depth)]).astype(jnp.bfloat16)
            term = jnp.dot(scaled, w[pl.ds(base, depth), :], preferred_element_type=jnp.float32)
            total = term if total is None else total + term
            exact = exact * exact
            folded = (exact[:, :128] + exact[:, 128:256]) + (exact[:, 256:384] + exact[:, 384:512])
            square = folded if square is None else square + folded
        return total, square

    def early_half(start, rows):
        total, square = half_product(start, rows, zh)
        acc[pl.ds(start, rows), :] = total
        squares[pl.ds(start, rows), :] = square

    def project(start, rows):
        total, square = half_product(start, rows, 1 - zh)
        total = total + acc[pl.ds(start, rows), :]
        square = jnp.sum(square + squares[pl.ds(start, rows), :], axis=1, keepdims=True)
        projected = total * lax.rsqrt(square / (8 * depth) + EPS)
        cosine = cosines[pl.ds(start, rows), :]
        sine = sines[pl.ds(start, rows), :]

        def head(index):
            return projected[:, index * HEAD : (index + 1) * HEAD]

        def rotated(index):
            return (head(index) * cosine + pltpu.roll(head(index), HEAD // 2, 1) * sine).astype(jnp.bfloat16)

        queries = jnp.concatenate([rotated(i) for i in range(QPG)], axis=0)
        return queries, rotated(QPG), head(QPG + 1).astype(jnp.bfloat16)

    def against(queries, keys):
        return lax.dot_general(queries, keys, (((1,), (1,)), ((), ())), preferred_element_type=jnp.float32)

    def attend(parts):
        highest = None
        for scores, _ in parts:
            top = jnp.max(scores, axis=1, keepdims=True)
            highest = top if highest is None else jnp.maximum(highest, top)
        total = None
        output = None
        for scores, values in parts:
            expo = jnp.exp2((scores - highest) * FACTOR)
            part_total = jnp.sum(expo, axis=1, keepdims=True)
            part_out = jnp.dot(expo.astype(jnp.bfloat16), values, preferred_element_type=jnp.float32)
            total = part_total if total is None else total + part_total
            output = part_out if output is None else output + part_out
        return (output / total).astype(jnp.bfloat16)

    def iota(shape, dim):
        return lax.broadcasted_iota(jnp.int32, shape, dim)

    def column_of(row):
        n = row.shape[1]
        square = jnp.where(iota((n, n), 0) == iota((n, n), 1), row.astype(jnp.float32), 0.0)
        return jnp.sum(square, axis=1, keepdims=True)

    def prepare():
        lengths = column_of(tail_len[...])
        block_pos = (iota((block_rows, 1), 0) + offset[0]).astype(jnp.float32)
        for start, rows, position in (
            (0, group_rows, prompt.shape[0] + lengths), (group_rows, block_rows, block_pos),
        ):
            angle = position * freq[...]
            cosines[pl.ds(start, rows), :] = jnp.cos(angle)
            sine = jnp.sin(angle)
            sines[pl.ds(start, rows), :] = jnp.where(iota(sine.shape, 1) < HEAD // 2, -sine, sine)

    def places():
        pages = table.shape[1]
        slots = pool.shape[0]
        page_column = column_of(table[...])
        matches = page_column == iota((pages, pages), 1).astype(jnp.float32)
        inverse = jnp.sum(jnp.where(matches, iota((pages, pages), 0).astype(jnp.float32), 0.0), axis=0, keepdims=True)
        spread_out = jnp.where(iota((pages, slots), 1) // PAGE == iota((pages, slots), 0), 1.0, 0.0)
        inverse = jnp.broadcast_to(inverse, (8, pages)).astype(jnp.bfloat16)
        row = jnp.dot(inverse, spread_out.astype(jnp.bfloat16), preferred_element_type=jnp.float32)
        place_of[...] = row * PAGE + (iota((8, slots), 1) % PAGE).astype(jnp.float32)

    def decode():
        queries, own_keys, own_values = project(0, group_rows)
        count = QPG * group_rows
        slots = pool.shape[0] // group_rows
        request = iota((count, 1), 0) % group_rows
        lengths = jnp.concatenate([column_of(tail_len[...])] * QPG, axis=0)
        first = (request * slots).astype(jnp.float32)
        place = place_of[0:1, :]
        tail_scores = against(queries, pool[:, :HEAD])
        tail_scores = jnp.where((place >= first) & (place < first + lengths), tail_scores, MASKED)
        own_scores = against(queries, own_keys)
        own_scores = jnp.where(iota((1, group_rows), 1) == request, own_scores, MASKED)
        output = attend((
            (against(queries, prompt[:, :HEAD]), prompt[:, HEAD:]),
            (tail_scores, pool[:, HEAD:]),
            (own_scores, own_values),
        ))
        for h in range(QPG):
            moved[0, :, h * HEAD : (h + 1) * HEAD] = output[h * group_rows : (h + 1) * group_rows]

    def hop_start(bit):
        return send(moved.at[bit], landed.at[bit], partner(bit))

    def hop_end(bit, copy):
        copy.wait_recv()
        take = (jnp.full((1, 1), mask[0], jnp.int32) >> bit) & 1
        moved[bit + 1, :, :] = jnp.where(take == 1, landed[bit], moved[bit])

    def block(index):
        start, rows = CHUNKS[index]
        first = start - group_rows
        queries, keys, values = project(start, rows)
        keys_new[pl.ds(first, rows), :] = keys
        values_new[pl.ds(first, rows), :] = values
        bias = jnp.where(iota((1, ctx.shape[0]), 1) < offset[0], 0.0, MASKED)
        parts = [(against(queries, ctx[:, :HEAD]) + bias, ctx[:, HEAD:])]
        seen = first + rows
        inside = against(queries, keys_new[pl.ds(0, seen), :])
        token = first + iota((QPG * rows, 1), 0) % rows
        inside = jnp.where(iota((1, seen), 1) <= token, inside, MASKED)
        parts.append((inside, values_new[pl.ds(0, seen), :]))
        output = attend(parts)
        for h in range(QPG):
            out_rows[pl.ds(first, rows), h * HEAD : (h + 1) * HEAD] = output[h * rows : (h + 1) * rows]
        view = pl.ds(first, rows)
        copy = pltpu.make_async_copy(out_rows.at[view], block_out.at[view], local_sem.at[6 + index])
        copy.start()
        return copy

    received = []
    copies_out = []
    prepare()
    places()
    received += forward_own(0)
    near = [None] * len(CHUNKS)
    far = [None] * len(CHUNKS)
    near[0] = spread(0)
    locals_[0].wait()
    locals_[1].wait()
    locals_[2].wait()
    for copy in received:
        copy.wait_recv()
    early_half(0, 32)
    far[0] = forward_far(0, near[0])
    fwd1 = forward_own(1)
    for copy in far[0]:
        copy.wait_recv()
    locals_[3].wait()
    locals_[4].wait()
    decode()
    locals_[5].wait()
    fwd2 = forward_own(2)
    hop = hop_start(0)
    for copy in fwd1:
        copy.wait_recv()
    early_half(32, 96)
    near[1] = spread(1)
    hop_end(0, hop)
    hop = hop_start(1)
    early_half(128, 96)
    far[1] = forward_far(1, near[1])
    for copy in far[1]:
        copy.wait_recv()
    hop_end(1, hop)
    hop = hop_start(2)
    copies_out.append(block(1))
    for copy in fwd2:
        copy.wait_recv()
    near[2] = spread(2)
    hop_end(2, hop)
    hop = hop_start(3)
    early_half(224, 96)
    far[2] = forward_far(2, near[2])
    for copy in far[2]:
        copy.wait_recv()
    hop_end(3, hop)
    hop = hop_start(4)
    copies_out.append(block(2))
    near[3] = spread(3)
    hop_end(4, hop)
    hop = hop_start(5)
    early_half(320, 96)
    far[3] = forward_far(3, near[3])
    for copy in far[3]:
        copy.wait_recv()
    hop_end(5, hop)
    copy = pltpu.make_async_copy(moved.at[HOPS], decode_out, local_sem.at[6])
    copy.start()
    copies_out.append(copy)
    copies_out.append(block(3))
    near[4] = spread(4)
    far[4] = forward_far(4, near[4])
    near[5] = spread(5)
    for copy in far[4]:
        copy.wait_recv()
    far[5] = forward_far(5, near[5])
    copies_out.append(block(4))
    for copy in far[5]:
        copy.wait_recv()
    copies_out.append(block(5))
    for copy in sent:
        copy.wait_send()
    for copy in copies_out:
        copy.wait()


def per_device(
    block_x, decode_x, gain, w_qkv, ctx_cache, prompt_cache, tail_pool, page_table, tail_len, block_offset, move_mask
):
    rows = block_x.shape[0] + decode_x.shape[0]
    depth = block_x.shape[1]
    frequency = np.power(THETA, -2.0 * np.arange(HEAD // 2) / HEAD).astype(np.float32)
    freq = jnp.asarray(np.concatenate([frequency, frequency])[None, :])
    hbm = pl.BlockSpec(memory_space=pl.ANY)
    vmem = pl.BlockSpec(memory_space=pltpu.VMEM)
    smem = pl.BlockSpec(memory_space=pltpu.SMEM)
    bf16, f32 = jnp.bfloat16, jnp.float32
    return pl.pallas_call(
        layer_kernel,
        out_shape=(
            jax.ShapeDtypeStruct(block_x.shape, bf16),
            jax.ShapeDtypeStruct(decode_x.shape, bf16),
        ),
        in_specs=[hbm, hbm, vmem, hbm, hbm, hbm, hbm, vmem, vmem, smem, smem, vmem],
        out_specs=(hbm, hbm),
        scratch_shapes=[
            pltpu.VMEM((8, rows, depth), bf16),
            pltpu.VMEM(w_qkv.shape, bf16),
            pltpu.VMEM(ctx_cache.shape, bf16),
            pltpu.VMEM(prompt_cache.shape, bf16),
            pltpu.VMEM(tail_pool.shape, bf16),
            pltpu.VMEM((8, tail_pool.shape[0]), f32),
            pltpu.VMEM((rows, w_qkv.shape[1]), f32),
            pltpu.VMEM((rows, 128), f32),
            pltpu.VMEM((rows, HEAD), f32),
            pltpu.VMEM((rows, HEAD), f32),
            pltpu.VMEM((block_x.shape[0], HEAD), bf16),
            pltpu.VMEM((block_x.shape[0], HEAD), bf16),
            pltpu.VMEM(block_x.shape, bf16),
            pltpu.VMEM((HOPS + 1,) + decode_x.shape, bf16),
            pltpu.VMEM((HOPS,) + decode_x.shape, bf16),
            pltpu.SemaphoreType.DMA((12,)),
            pltpu.SemaphoreType.DMA((64,)),
            pltpu.SemaphoreType.DMA((64,)),
        ],
        compiler_params=pltpu.CompilerParams(
            collective_id=0, has_side_effects=True, vmem_limit_bytes=56 * 2**20
        ),
        name="layer",
    )(
        block_x, decode_x, gain.astype(f32)[None, :], w_qkv, ctx_cache, prompt_cache, tail_pool,
        page_table, tail_len, block_offset, move_mask, freq,
    )


def solution(mesh):
    in_specs = (
        P("req", "tp"),
        P("req", "tp"),
        P(),
        P(None, "tp"),
        P("req", "tp"),
        P("req", "tp"),
        P("req", "tp"),
        P("req", None),
        P("req", None),
        P("req"),
        P(),
    )
    out_specs = (P("req", "tp"), P("req", "tp"))
    return jax.shard_map(
        per_device, mesh=mesh, in_specs=in_specs, out_specs=out_specs, check_vma=False
    )
```

```python
import functools
import math

import jax
import jax.numpy as jnp
import numpy as np
from jax import lax
from jax.experimental import pallas as pl
from jax.experimental.pallas import tpu as pltpu
from jax.sharding import PartitionSpec as P

HEAD = 128
QPG = 4
EPS = 1e-05
THETA = 1000000.0
PAGE = 16
MESH = pl.DeviceIdType.MESH
CHUNKS = ((0, 32), (32, 96), (128, 128), (256, 128), (384, 32))
OWN = ((0, 32), (32, 192), (224, 192))
HOPS = 6
MASKED = -1e30
FACTOR = HEAD ** -0.5 * math.log2(math.e)


def where_am_i():
    req = lax.axis_index("req")
    tp = lax.axis_index("tp")
    return req, tp, tp // 2, tp % 2


def layer_kernel(
    block_x, decode_x, gain, w_hbm, ctx_hbm, prompt_hbm, pool_hbm, table, tail_len, offset, mask, freq,
    block_out, decode_out,
    gathered, w, ctx, prompt, pool, place_of, acc, squares, cosines, sines, keys_new, values_new,
    out_rows, moved, landed, local_sem, send_sem, recv_sem,
):
    req, tp, y, zh = where_am_i()
    group_rows = decode_x.shape[0]
    block_rows = block_x.shape[0]
    depth = decode_x.shape[1]
    opposite = (req, tp + 1 - 2 * zh)

    def along_y(step):
        return (req, ((y + step + 4) % 4) * 2 + zh)

    def partner(bit):
        here = (req // (1 << bit)) % 2
        return (req + (1 - 2 * here) * (1 << bit), tp)

    peers = [opposite, along_y(1), along_y(-1)] + [partner(bit) for bit in range(HOPS)]
    barrier = pltpu.get_barrier_semaphore()
    for peer in peers:
        pl.semaphore_signal(barrier, inc=1, device_id=peer, device_id_type=MESH)

    locals_ = [
        pltpu.make_async_copy(decode_x, gathered.at[tp, pl.ds(0, group_rows)], local_sem.at[0]),
        pltpu.make_async_copy(block_x, gathered.at[tp, pl.ds(group_rows, block_rows)], local_sem.at[1]),
        pltpu.make_async_copy(w_hbm, w, local_sem.at[2]),
        pltpu.make_async_copy(pool_hbm, pool, local_sem.at[3]),
        pltpu.make_async_copy(prompt_hbm, prompt, local_sem.at[4]),
        pltpu.make_async_copy(ctx_hbm, ctx, local_sem.at[5]),
    ]
    for copy in locals_:
        copy.start()
    pl.semaphore_wait(barrier, len(peers))

    sent = []

    def send(source, target, device):
        index = len(sent)
        copy = pltpu.make_async_remote_copy(
            src_ref=source, dst_ref=target, send_sem=send_sem.at[index], recv_sem=recv_sem.at[index],
            device_id=device, device_id_type=MESH,
        )
        copy.start()
        sent.append(copy)
        return copy

    def own_rows(start, rows):
        if start < group_rows:
            return decode_x.at[pl.ds(start, rows)]
        return block_x.at[pl.ds(start - group_rows, rows)]

    directions = (1, -1)
    across = [send(own_rows(s, n), gathered.at[tp, pl.ds(s, n)], opposite) for s, n in CHUNKS]
    beside = [
        [send(own_rows(s, n), gathered.at[tp, pl.ds(s, n)], along_y(d)) for d in directions] for s, n in OWN
    ]

    def forward(near, start, rows, half):
        copies = []
        for which, d in enumerate(directions):
            near[which].wait_recv()
            slot = ((y - d + 4) % 4) * 2 + half
            view = gathered.at[slot, pl.ds(start + which * (rows // 2), rows // 2)]
            copies.append(send(view, view, along_y(d)))
        return copies

    def forward_own(index):
        return forward(beside[index], OWN[index][0], OWN[index][1], zh)

    def spread(index):
        start, rows = CHUNKS[index]
        across[index].wait_recv()
        view = gathered.at[tp + 1 - 2 * zh, pl.ds(start, rows)]
        return [send(view, view, along_y(d)) for d in directions]

    def forward_far(index, near):
        return forward(near, CHUNKS[index][0], CHUNKS[index][1], 1 - zh)

    def half_product(start, rows, half):
        total = None
        square = None
        for j in range(4):
            slot = 2 * j + half
            exact = gathered[slot, pl.ds(start, rows), :].astype(jnp.float32)
            base = pl.multiple_of(slot * depth, depth)
            scaled = (exact * gain[pl.ds(base, depth)].astype(jnp.float32)[None, :]).astype(jnp.bfloat16)
            term = jnp.dot(scaled, w[pl.ds(base, depth), :], preferred_element_type=jnp.float32)
            total = term if total is None else total + term
            exact = exact * exact
            folded = (exact[:, :128] + exact[:, 128:256]) + (exact[:, 256:384] + exact[:, 384:512])
            square = folded if square is None else square + folded
        return total, square

    def early_half(start, rows):
        total, square = half_product(start, rows, zh)
        acc[pl.ds(start, rows), :] = total
        squares[pl.ds(start, rows), :] = square

    def project(start, rows):
        total, square = half_product(start, rows, 1 - zh)
        total = total + acc[pl.ds(start, rows), :]
        square = jnp.sum(square + squares[pl.ds(start, rows), :], axis=1, keepdims=True)
        projected = total * lax.rsqrt(square / (8 * depth) + EPS)
        cosine = cosines[pl.ds(start, rows), :]
        sine = sines[pl.ds(start, rows), :]

        def head(index):
            return projected[:, index * HEAD : (index + 1) * HEAD]

        def rotated(index):
            return (head(index) * cosine + pltpu.roll(head(index), HEAD // 2, 1) * sine).astype(jnp.bfloat16)

        queries = jnp.concatenate([rotated(i) for i in range(QPG)], axis=0)
        return queries, rotated(QPG), head(QPG + 1).astype(jnp.bfloat16)

    def against(queries, keys):
        return lax.dot_general(queries, keys, (((1,), (1,)), ((), ())), preferred_element_type=jnp.float32)

    def attend(parts):
        highest = None
        for scores, _ in parts:
            top = jnp.max(scores, axis=1, keepdims=True)
            highest = top if highest is None else jnp.maximum(highest, top)
        total = None
        output = None
        for scores, values in parts:
            expo = jnp.exp2((scores - highest) * FACTOR)
            part_total = jnp.sum(expo, axis=1, keepdims=True)
            part_out = jnp.dot(expo.astype(jnp.bfloat16), values, preferred_element_type=jnp.float32)
            total = part_total if total is None else total + part_total
            output = part_out if output is None else output + part_out
        return (output / total).astype(jnp.bfloat16)

    def iota(shape, dim):
        return lax.broadcasted_iota(jnp.int32, shape, dim)

    def column_of(row):
        n = row.shape[1]
        square = jnp.where(iota((n, n), 0) == iota((n, n), 1), row.astype(jnp.float32), 0.0)
        return jnp.sum(square, axis=1, keepdims=True)

    def prepare():
        lengths = column_of(tail_len[...])
        block_pos = (iota((block_rows, 1), 0) + offset[0]).astype(jnp.float32)
        for start, rows, position in (
            (0, group_rows, prompt.shape[0] + lengths), (group_rows, block_rows, block_pos),
        ):
            angle = position * freq[...]
            cosines[pl.ds(start, rows), :] = jnp.cos(angle)
            sine = jnp.sin(angle)
            sines[pl.ds(start, rows), :] = jnp.where(iota(sine.shape, 1) < HEAD // 2, -sine, sine)

    def places():
        pages = table.shape[1]
        slots = pool.shape[0]
        page_column = column_of(table[...])
        matches = page_column == iota((pages, pages), 1).astype(jnp.float32)
        inverse = jnp.sum(jnp.where(matches, iota((pages, pages), 0).astype(jnp.float32), 0.0), axis=0, keepdims=True)
        spread_out = jnp.where(iota((pages, slots), 1) // PAGE == iota((pages, slots), 0), 1.0, 0.0)
        inverse = jnp.broadcast_to(inverse, (8, pages)).astype(jnp.bfloat16)
        row = jnp.dot(inverse, spread_out.astype(jnp.bfloat16), preferred_element_type=jnp.float32)
        place_of[...] = row * PAGE + (iota((8, slots), 1) % PAGE).astype(jnp.float32)

    def decode():
        queries, own_keys, own_values = project(0, group_rows)
        count = QPG * group_rows
        slots = pool.shape[0] // group_rows
        request = iota((count, 1), 0) % group_rows
        lengths = jnp.concatenate([column_of(tail_len[...])] * QPG, axis=0)
        first = (request * slots).astype(jnp.float32)
        place = place_of[0:1, :]
        tail_scores = against(queries, pool[:, :HEAD])
        tail_scores = jnp.where((place >= first) & (place < first + lengths), tail_scores, MASKED)
        own_scores = against(queries, own_keys)
        own_scores = jnp.where(iota((1, group_rows), 1) == request, own_scores, MASKED)
        output = attend((
            (against(queries, prompt[:, :HEAD]), prompt[:, HEAD:]),
            (tail_scores, pool[:, HEAD:]),
            (own_scores, own_values),
        ))
        for h in range(QPG):
            moved[0, :, h * HEAD : (h + 1) * HEAD] = output[h * group_rows : (h + 1) * group_rows]

    def hop_start(bit):
        return send(moved.at[bit], landed.at[bit], partner(bit))

    def hop_end(bit, copy):
        copy.wait_recv()
        take = (jnp.full((1, 1), mask[0], jnp.int32) >> bit) & 1
        moved[bit + 1, :, :] = jnp.where(take == 1, landed[bit], moved[bit])

    def block(index):
        start, rows = CHUNKS[index]
        first = start - group_rows
        queries, keys, values = project(start, rows)
        keys_new[pl.ds(first, rows), :] = keys
        values_new[pl.ds(first, rows), :] = values
        bias = jnp.where(iota((1, ctx.shape[0]), 1) < offset[0], 0.0, MASKED)
        parts = [(against(queries, ctx[:, :HEAD]) + bias, ctx[:, HEAD:])]
        seen = first + rows
        inside = against(queries, keys_new[pl.ds(0, seen), :])
        token = first + iota((QPG * rows, 1), 0) % rows
        inside = jnp.where(iota((1, seen), 1) <= token, inside, MASKED)
        parts.append((inside, values_new[pl.ds(0, seen), :]))
        output = attend(parts)
        for h in range(QPG):
            out_rows[pl.ds(first, rows), h * HEAD : (h + 1) * HEAD] = output[h * rows : (h + 1) * rows]
        view = pl.ds(first, rows)
        copy = pltpu.make_async_copy(out_rows.at[view], block_out.at[view], local_sem.at[6 + index])
        copy.start()
        return copy

    copies_out = []

    def arrived(copies):
        for copy in copies:
            copy.wait_recv()

    prepare()
    places()
    own0 = forward_own(0)
    near0 = spread(0)
    own1 = forward_own(1)
    for copy in locals_[:3]:
        copy.wait()
    arrived(own0)
    early_half(0, 32)
    far0 = forward_far(0, near0)
    own2 = forward_own(2)
    arrived(own1)
    early_half(32, 192)
    for copy in locals_[3:]:
        copy.wait()
    arrived(far0)
    decode()
    hop = [hop_start(0)]

    def hop_on():
        bit = len(hop) - 1
        if bit >= HOPS:
            return
        hop_end(bit, hop[bit])
        if bit + 1 < HOPS:
            hop.append(hop_start(bit + 1))
            return
        hop.append(pltpu.make_async_copy(moved.at[HOPS], decode_out, local_sem.at[6]))
        hop[-1].start()
        copies_out.append(hop[-1])

    last = len(CHUNKS) - 1
    near = {1: spread(1)}
    hop_on()
    arrived(own2)
    early_half(224, 192)
    near[2] = spread(2)
    hop_on()
    far = {1: forward_far(1, near[1])}
    hop_on()
    for k in range(3, last + 1):
        near[k] = spread(k)
        hop_on()
        if k == last:
            far[k - 1] = forward_far(k - 1, near[k - 1])
        arrived(far[k - 2])
        copies_out.append(block(k - 2))
        if k < last:
            far[k - 1] = forward_far(k - 1, near[k - 1])
        hop_on()
    far[last] = forward_far(last, near[last])
    for k in (last - 1, last):
        arrived(far[k])
        copies_out.append(block(k))
    for copy in sent:
        copy.wait_send()
    for copy in copies_out:
        copy.wait()


def finish_kernel(block_in, decode_in, block_out, decode_out):
    block_out[...] = block_in[...]
    decode_out[...] = decode_in[...]


def per_device(
    block_x, decode_x, gain, w_qkv, ctx_cache, prompt_cache, tail_pool, page_table, tail_len, block_offset, move_mask
):
    rows = block_x.shape[0] + decode_x.shape[0]
    depth = block_x.shape[1]
    frequency = np.power(THETA, -2.0 * np.arange(HEAD // 2) / HEAD).astype(np.float32)
    freq = jnp.asarray(np.concatenate([frequency, frequency])[None, :])
    hbm = pl.BlockSpec(memory_space=pl.ANY)
    vmem = pl.BlockSpec(memory_space=pltpu.VMEM)
    smem = pl.BlockSpec(memory_space=pltpu.SMEM)
    bf16, f32 = jnp.bfloat16, jnp.float32
    outputs = pl.pallas_call(
        layer_kernel,
        out_shape=(
            jax.ShapeDtypeStruct(block_x.shape, bf16),
            jax.ShapeDtypeStruct(decode_x.shape, bf16),
        ),
        in_specs=[hbm, hbm, vmem, hbm, hbm, hbm, hbm, vmem, vmem, smem, smem, vmem],
        out_specs=(hbm, hbm),
        scratch_shapes=[
            pltpu.VMEM((8, rows, depth), bf16),
            pltpu.VMEM(w_qkv.shape, bf16),
            pltpu.VMEM(ctx_cache.shape, bf16),
            pltpu.VMEM(prompt_cache.shape, bf16),
            pltpu.VMEM(tail_pool.shape, bf16),
            pltpu.VMEM((8, tail_pool.shape[0]), f32),
            pltpu.VMEM((rows, w_qkv.shape[1]), f32),
            pltpu.VMEM((rows, 128), f32),
            pltpu.VMEM((rows, HEAD), f32),
            pltpu.VMEM((rows, HEAD), f32),
            pltpu.VMEM((block_x.shape[0], HEAD), bf16),
            pltpu.VMEM((block_x.shape[0], HEAD), bf16),
            pltpu.VMEM(block_x.shape, bf16),
            pltpu.VMEM((HOPS + 1,) + decode_x.shape, bf16),
            pltpu.VMEM((HOPS,) + decode_x.shape, bf16),
            pltpu.SemaphoreType.DMA((12,)),
            pltpu.SemaphoreType.DMA((64,)),
            pltpu.SemaphoreType.DMA((64,)),
        ],
        compiler_params=pltpu.CompilerParams(
            collective_id=0, has_side_effects=True, vmem_limit_bytes=56 * 2**20
        ),
        name="layer",
    )(
        block_x, decode_x, gain, w_qkv, ctx_cache, prompt_cache, tail_pool,
        page_table, tail_len, block_offset, move_mask, freq,
    )
    return pl.pallas_call(
        finish_kernel,
        out_shape=[jax.ShapeDtypeStruct(o.shape, o.dtype) for o in outputs],
        in_specs=[vmem, vmem],
        out_specs=[vmem, vmem],
        name="finish",
    )(*outputs)


def solution(mesh):
    in_specs = (
        P("req", "tp"),
        P("req", "tp"),
        P(),
        P(None, "tp"),
        P("req", "tp"),
        P("req", "tp"),
        P("req", "tp"),
        P("req", None),
        P("req", None),
        P("req"),
        P(),
    )
    out_specs = (P("req", "tp"), P("req", "tp"))
    return jax.shard_map(
        per_device, mesh=mesh, in_specs=in_specs, out_specs=out_specs, check_vma=False
    )
```

```python
import functools
import math

import jax
import jax.numpy as jnp
import numpy as np
from jax import lax
from jax.experimental import pallas as pl
from jax.experimental.pallas import tpu as pltpu
from jax.sharding import PartitionSpec as P

HEAD = 128
QPG = 4
EPS = 1e-05
THETA = 1000000.0
PAGE = 16
MESH = pl.DeviceIdType.MESH
CHUNKS = ((0, 32), (32, 64), (96, 96), (192, 96), (288, 128))
OWN = ((0, 32), (32, 192), (224, 192))
HOPS = 6
MASKED = -1e30
FACTOR = HEAD ** -0.5 * math.log2(math.e)


def where_am_i():
    req = lax.axis_index("req")
    tp = lax.axis_index("tp")
    return req, tp, tp // 2, tp % 2


def layer_kernel(
    block_x, decode_x, gain, w_hbm, ctx_hbm, prompt_hbm, pool_hbm, table, tail_len, offset, mask, freq,
    block_out, decode_out,
    gathered, w, ctx, prompt, pool, place_of, acc, squares, cosines, sines, keys_new, values_new,
    out_rows, moved, landed, local_sem, send_sem, recv_sem,
):
    req, tp, y, zh = where_am_i()
    group_rows = decode_x.shape[0]
    block_rows = block_x.shape[0]
    depth = decode_x.shape[1]
    opposite = (req, tp + 1 - 2 * zh)

    def along_y(step):
        return (req, ((y + step + 4) % 4) * 2 + zh)

    def partner(bit):
        here = (req // (1 << bit)) % 2
        return (req + (1 - 2 * here) * (1 << bit), tp)

    peers = [opposite, along_y(1), along_y(-1)] + [partner(bit) for bit in range(HOPS)]
    barrier = pltpu.get_barrier_semaphore()
    for peer in peers:
        pl.semaphore_signal(barrier, inc=1, device_id=peer, device_id_type=MESH)

    locals_ = [
        pltpu.make_async_copy(decode_x, gathered.at[tp, pl.ds(0, group_rows)], local_sem.at[0]),
        pltpu.make_async_copy(block_x, gathered.at[tp, pl.ds(group_rows, block_rows)], local_sem.at[1]),
        pltpu.make_async_copy(w_hbm, w, local_sem.at[2]),
        pltpu.make_async_copy(pool_hbm, pool, local_sem.at[3]),
        pltpu.make_async_copy(prompt_hbm, prompt, local_sem.at[4]),
        pltpu.make_async_copy(ctx_hbm, ctx, local_sem.at[5]),
    ]
    for copy in locals_:
        copy.start()
    pl.semaphore_wait(barrier, len(peers))

    sent = []

    def send(source, target, device):
        index = len(sent)
        copy = pltpu.make_async_remote_copy(
            src_ref=source, dst_ref=target, send_sem=send_sem.at[index], recv_sem=recv_sem.at[index],
            device_id=device, device_id_type=MESH,
        )
        copy.start()
        sent.append(copy)
        return copy

    def own_rows(start, rows):
        if start < group_rows:
            return decode_x.at[pl.ds(start, rows)]
        return block_x.at[pl.ds(start - group_rows, rows)]

    directions = (1, -1)
    across = [send(own_rows(s, n), gathered.at[tp, pl.ds(s, n)], opposite) for s, n in CHUNKS]
    beside = [
        [send(own_rows(s, n), gathered.at[tp, pl.ds(s, n)], along_y(d)) for d in directions] for s, n in OWN
    ]

    def forward(near, start, rows, half):
        copies = []
        for which, d in enumerate(directions):
            near[which].wait_recv()
            slot = ((y - d + 4) % 4) * 2 + half
            view = gathered.at[slot, pl.ds(start + which * (rows // 2), rows // 2)]
            copies.append(send(view, view, along_y(d)))
        return copies

    def forward_own(index):
        return forward(beside[index], OWN[index][0], OWN[index][1], zh)

    def spread(index):
        start, rows = CHUNKS[index]
        across[index].wait_recv()
        view = gathered.at[tp + 1 - 2 * zh, pl.ds(start, rows)]
        return [send(view, view, along_y(d)) for d in directions]

    def forward_far(index, near):
        return forward(near, CHUNKS[index][0], CHUNKS[index][1], 1 - zh)

    def half_product(start, rows, half):
        total = None
        square = None
        for j in range(4):
            slot = 2 * j + half
            exact = gathered[slot, pl.ds(start, rows), :].astype(jnp.float32)
            base = pl.multiple_of(slot * depth, depth)
            scaled = (exact * gain[pl.ds(base, depth)].astype(jnp.float32)[None, :]).astype(jnp.bfloat16)
            term = jnp.dot(scaled, w[pl.ds(base, depth), :], preferred_element_type=jnp.float32)
            total = term if total is None else total + term
            exact = exact * exact
            folded = (exact[:, :128] + exact[:, 128:256]) + (exact[:, 256:384] + exact[:, 384:512])
            square = folded if square is None else square + folded
        return total, square

    def early_half(start, rows):
        total, square = half_product(start, rows, zh)
        acc[pl.ds(start, rows), :] = total
        squares[pl.ds(start, rows), :] = square

    def project(start, rows):
        total, square = half_product(start, rows, 1 - zh)
        total = total + acc[pl.ds(start, rows), :]
        square = jnp.sum(square + squares[pl.ds(start, rows), :], axis=1, keepdims=True)
        projected = total * lax.rsqrt(square / (8 * depth) + EPS)
        cosine = cosines[pl.ds(start, rows), :]
        sine = sines[pl.ds(start, rows), :]

        def head(index):
            return projected[:, index * HEAD : (index + 1) * HEAD]

        def rotated(index):
            return (head(index) * cosine + pltpu.roll(head(index), HEAD // 2, 1) * sine).astype(jnp.bfloat16)

        queries = jnp.concatenate([rotated(i) for i in range(QPG)], axis=0)
        return queries, rotated(QPG), head(QPG + 1).astype(jnp.bfloat16)

    def against(queries, keys):
        return lax.dot_general(queries, keys, (((1,), (1,)), ((), ())), preferred_element_type=jnp.float32)

    def attend(parts):
        highest = None
        for scores, _ in parts:
            top = jnp.max(scores, axis=1, keepdims=True)
            highest = top if highest is None else jnp.maximum(highest, top)
        total = None
        output = None
        for scores, values in parts:
            expo = jnp.exp2((scores - highest) * FACTOR)
            part_total = jnp.sum(expo, axis=1, keepdims=True)
            part_out = jnp.dot(expo.astype(jnp.bfloat16), values, preferred_element_type=jnp.float32)
            total = part_total if total is None else total + part_total
            output = part_out if output is None else output + part_out
        return (output / total).astype(jnp.bfloat16)

    def iota(shape, dim):
        return lax.broadcasted_iota(jnp.int32, shape, dim)

    def column_of(row):
        n = row.shape[1]
        square = jnp.where(iota((n, n), 0) == iota((n, n), 1), row.astype(jnp.float32), 0.0)
        return jnp.sum(square, axis=1, keepdims=True)

    def prepare():
        lengths = column_of(tail_len[...])
        block_pos = (iota((block_rows, 1), 0) + offset[0]).astype(jnp.float32)
        for start, rows, position in (
            (0, group_rows, prompt.shape[0] + lengths), (group_rows, block_rows, block_pos),
        ):
            angle = position * freq[...]
            cosines[pl.ds(start, rows), :] = jnp.cos(angle)
            sine = jnp.sin(angle)
            sines[pl.ds(start, rows), :] = jnp.where(iota(sine.shape, 1) < HEAD // 2, -sine, sine)

    def places():
        pages = table.shape[1]
        slots = pool.shape[0]
        page_column = column_of(table[...])
        matches = page_column == iota((pages, pages), 1).astype(jnp.float32)
        inverse = jnp.sum(jnp.where(matches, iota((pages, pages), 0).astype(jnp.float32), 0.0), axis=0, keepdims=True)
        spread_out = jnp.where(iota((pages, slots), 1) // PAGE == iota((pages, slots), 0), 1.0, 0.0)
        inverse = jnp.broadcast_to(inverse, (8, pages)).astype(jnp.bfloat16)
        row = jnp.dot(inverse, spread_out.astype(jnp.bfloat16), preferred_element_type=jnp.float32)
        place_of[...] = row * PAGE + (iota((8, slots), 1) % PAGE).astype(jnp.float32)

    def decode():
        queries, own_keys, own_values = project(0, group_rows)
        count = QPG * group_rows
        slots = pool.shape[0] // group_rows
        request = iota((count, 1), 0) % group_rows
        lengths = jnp.concatenate([column_of(tail_len[...])] * QPG, axis=0)
        first = (request * slots).astype(jnp.float32)
        place = place_of[0:1, :]
        tail_scores = against(queries, pool[:, :HEAD])
        tail_scores = jnp.where((place >= first) & (place < first + lengths), tail_scores, MASKED)
        own_scores = against(queries, own_keys)
        own_scores = jnp.where(iota((1, group_rows), 1) == request, own_scores, MASKED)
        output = attend((
            (against(queries, prompt[:, :HEAD]), prompt[:, HEAD:]),
            (tail_scores, pool[:, HEAD:]),
            (own_scores, own_values),
        ))
        for h in range(QPG):
            moved[0, :, h * HEAD : (h + 1) * HEAD] = output[h * group_rows : (h + 1) * group_rows]

    def hop_start(bit):
        return send(moved.at[bit], landed.at[bit], partner(bit))

    def hop_end(bit, copy):
        copy.wait_recv()
        take = (jnp.full((1, 1), mask[0], jnp.int32) >> bit) & 1
        moved[bit + 1, :, :] = jnp.where(take == 1, landed[bit], moved[bit])

    def block(index):
        start, rows = CHUNKS[index]
        first = start - group_rows
        queries, keys, values = project(start, rows)
        keys_new[pl.ds(first, rows), :] = keys
        values_new[pl.ds(first, rows), :] = values
        bias = jnp.where(iota((1, ctx.shape[0]), 1) < offset[0], 0.0, MASKED)
        parts = [(against(queries, ctx[:, :HEAD]) + bias, ctx[:, HEAD:])]
        seen = first + rows
        inside = against(queries, keys_new[pl.ds(0, seen), :])
        token = first + iota((QPG * rows, 1), 0) % rows
        inside = jnp.where(iota((1, seen), 1) <= token, inside, MASKED)
        parts.append((inside, values_new[pl.ds(0, seen), :]))
        output = attend(parts)
        for h in range(QPG):
            out_rows[pl.ds(first, rows), h * HEAD : (h + 1) * HEAD] = output[h * rows : (h + 1) * rows]
        view = pl.ds(first, rows)
        copy = pltpu.make_async_copy(out_rows.at[view], block_out.at[view], local_sem.at[6 + index])
        copy.start()
        return copy

    copies_out = []

    def arrived(copies):
        for copy in copies:
            copy.wait_recv()

    prepare()
    places()
    own0 = forward_own(0)
    near0 = spread(0)
    own1 = forward_own(1)
    for copy in locals_[:3]:
        copy.wait()
    arrived(own0)
    early_half(0, 32)
    far0 = forward_far(0, near0)
    own2 = forward_own(2)
    arrived(own1)
    early_half(32, 192)
    for copy in locals_[3:]:
        copy.wait()
    arrived(far0)
    decode()
    hop = [hop_start(0)]

    def hop_on():
        bit = len(hop) - 1
        if bit >= HOPS:
            return
        hop_end(bit, hop[bit])
        if bit + 1 < HOPS:
            hop.append(hop_start(bit + 1))
            return
        hop.append(pltpu.make_async_copy(moved.at[HOPS], decode_out, local_sem.at[6]))
        hop[-1].start()
        copies_out.append(hop[-1])

    last = len(CHUNKS) - 1
    near = {1: spread(1)}
    hop_on()
    arrived(own2)
    early_half(224, 192)
    near[2] = spread(2)
    hop_on()
    far = {1: forward_far(1, near[1])}
    hop_on()
    for k in range(3, last + 1):
        near[k] = spread(k)
        hop_on()
        if k == last:
            far[k - 1] = forward_far(k - 1, near[k - 1])
        arrived(far[k - 2])
        copies_out.append(block(k - 2))
        if k < last:
            far[k - 1] = forward_far(k - 1, near[k - 1])
        hop_on()
    far[last] = forward_far(last, near[last])
    for k in (last - 1, last):
        arrived(far[k])
        copies_out.append(block(k))
    for copy in sent:
        copy.wait_send()
    for copy in copies_out:
        copy.wait()


def finish_kernel(block_in, decode_in, block_out, decode_out):
    block_out[...] = block_in[...]
    decode_out[...] = decode_in[...]


def per_device(
    block_x, decode_x, gain, w_qkv, ctx_cache, prompt_cache, tail_pool, page_table, tail_len, block_offset, move_mask
):
    rows = block_x.shape[0] + decode_x.shape[0]
    depth = block_x.shape[1]
    frequency = np.power(THETA, -2.0 * np.arange(HEAD // 2) / HEAD).astype(np.float32)
    freq = jnp.asarray(np.concatenate([frequency, frequency])[None, :])
    hbm = pl.BlockSpec(memory_space=pl.ANY)
    vmem = pl.BlockSpec(memory_space=pltpu.VMEM)
    smem = pl.BlockSpec(memory_space=pltpu.SMEM)
    bf16, f32 = jnp.bfloat16, jnp.float32
    outputs = pl.pallas_call(
        layer_kernel,
        out_shape=(
            jax.ShapeDtypeStruct(block_x.shape, bf16),
            jax.ShapeDtypeStruct(decode_x.shape, bf16),
        ),
        in_specs=[hbm, hbm, vmem, hbm, hbm, hbm, hbm, vmem, vmem, smem, smem, vmem],
        out_specs=(hbm, hbm),
        scratch_shapes=[
            pltpu.VMEM((8, rows, depth), bf16),
            pltpu.VMEM(w_qkv.shape, bf16),
            pltpu.VMEM(ctx_cache.shape, bf16),
            pltpu.VMEM(prompt_cache.shape, bf16),
            pltpu.VMEM(tail_pool.shape, bf16),
            pltpu.VMEM((8, tail_pool.shape[0]), f32),
            pltpu.VMEM((rows, w_qkv.shape[1]), f32),
            pltpu.VMEM((rows, 128), f32),
            pltpu.VMEM((rows, HEAD), f32),
            pltpu.VMEM((rows, HEAD), f32),
            pltpu.VMEM((block_x.shape[0], HEAD), bf16),
            pltpu.VMEM((block_x.shape[0], HEAD), bf16),
            pltpu.VMEM(block_x.shape, bf16),
            pltpu.VMEM((HOPS + 1,) + decode_x.shape, bf16),
            pltpu.VMEM((HOPS,) + decode_x.shape, bf16),
            pltpu.SemaphoreType.DMA((12,)),
            pltpu.SemaphoreType.DMA((64,)),
            pltpu.SemaphoreType.DMA((64,)),
        ],
        compiler_params=pltpu.CompilerParams(
            collective_id=0, has_side_effects=True, vmem_limit_bytes=56 * 2**20
        ),
        name="layer",
    )(
        block_x, decode_x, gain, w_qkv, ctx_cache, prompt_cache, tail_pool,
        page_table, tail_len, block_offset, move_mask, freq,
    )
    return pl.pallas_call(
        finish_kernel,
        out_shape=[jax.ShapeDtypeStruct(o.shape, o.dtype) for o in outputs],
        in_specs=[vmem, vmem],
        out_specs=[vmem, vmem],
        name="finish",
    )(*outputs)


def solution(mesh):
    in_specs = (
        P("req", "tp"),
        P("req", "tp"),
        P(),
        P(None, "tp"),
        P("req", "tp"),
        P("req", "tp"),
        P("req", "tp"),
        P("req", None),
        P("req", None),
        P("req"),
        P(),
    )
    out_specs = (P("req", "tp"), P("req", "tp"))
    return jax.shard_map(
        per_device, mesh=mesh, in_specs=in_specs, out_specs=out_specs, check_vma=False
    )
```
